512 devices in a mesh: dp: 16 (over z_hi, y), expert: 32 (over x, z_lo, core).
Axes of the slice: x: 4, y: 8, z: 8 (z_hi: 2, z_lo: 4; z = z_hi * 4 + z_lo), core: 2. Of those that a mesh axis runs over, the one named last changes fastest.
Arguments:
- layer_input: bfloat16 [65536, 640], P(('dp', 'expert')), may hold values from -6 to 6
- output_grad: bfloat16 [65536, 640], P(('dp', 'expert')), may hold values from -6 to 6
- gate_weights: float32 [65536, 2], P(('dp', 'expert')), may hold values from 0.1 to 1
- expert_ids: int32 [65536, 2], P(('dp', 'expert')), may hold values from 0 to 31, as said below
- slot_positions: int32 [65536, 2], P(('dp', 'expert')), may hold values from 0 to 5, as said below
- keep_mask: int32 [65536, 2], P(('dp', 'expert')), may hold values from 0 to 1, as said below
- weight_in: bfloat16 [32, 640, 5120], P('expert', None, 'dp'), may hold values from -0.25 to 0.25
- weight_out: bfloat16 [32, 5120, 640], P('expert', 'dp'), may hold values from -0.078125 to 0.078125
Outputs:
- input_grad: bfloat16 [65536, 640], P(('dp', 'expert'))
- weight_in_grad: bfloat16 [32, 640, 5120], P('expert', None, 'dp')
- weight_out_grad: bfloat16 [32, 5120, 640], P('expert', 'dp')
The draws below stay inside these ranges and needn't reach their ends.
Inputs may be any that keep to these rules, and one draw needn't show every extreme that they name: `expert_ids`: a token's two experts differ. `slot_positions`: within the tokens of one device, taken in order with a token's first choice before its second, the choices naming one expert take positions 0, 1, 2 and so on; a choice at position 6 or beyond is dropped and has slot 0; kept choices of one device and expert have distinct slots. `keep_mask`: 1 exactly where the choice's position is below 6.
All inputs are finite; a program needn't handle non-finite values.
Results may differ from the reference program's by a relative error of at most 0.015.
Values may be sent and summed in bfloat16 or wider, within the bound.
A program may use at most 64 MiB of HBM per device.

```python
import jax
import jax.numpy as jnp
from jax import lax

D = 640
FF = 5120
TOK_DEV = 128
EXPERTS = 32
CAP = 6
TOKENS = 65536
N_DP = 16


def routing_table(key):
    blocks = TOKENS // TOK_DEV
    key_hot = jax.random.fold_in(key, 11)
    key_choose = jax.random.fold_in(key, 12)
    key_first = jax.random.fold_in(key, 13)
    key_offset = jax.random.fold_in(key, 14)
    hot_expert = jax.random.randint(key_hot, (blocks,), 0, EXPERTS, dtype=jnp.int32)
    hot_tokens = jnp.repeat(hot_expert, TOK_DEV)
    choose = jax.random.randint(key_choose, (TOKENS,), 0, 4, dtype=jnp.int32)
    random_first = jax.random.randint(key_first, (TOKENS,), 0, EXPERTS, dtype=jnp.int32)
    first_pick = jnp.where(choose == 0, hot_tokens, random_first)
    offset = jax.random.randint(key_offset, (TOKENS,), 1, EXPERTS, dtype=jnp.int32)
    second = (first_pick + offset) % EXPERTS
    chosen = jnp.stack([first_pick, second], axis=1).astype(jnp.int32)
    flat_choice = chosen.reshape(blocks, 2 * TOK_DEV)
    onehot = (flat_choice[:, :, None] == jnp.arange(EXPERTS, dtype=jnp.int32)[None, None, :]).astype(jnp.int32)
    earlier = jnp.cumsum(onehot, axis=1) - onehot
    position = jnp.sum(earlier * onehot, axis=2).reshape(TOKENS, 2)
    keeping = (position < CAP).astype(jnp.int32)
    slots = jnp.where(position < CAP, position, 0).astype(jnp.int32)
    return (chosen, slots, keeping)


def draw_expert_ids(key, part):
    return routing_table(key)[0]


def draw_slot_positions(key, part):
    return routing_table(key)[1]


def draw_keep_mask(key, part):
    return routing_table(key)[2]


def block_levels(key, shape, shards, low, high):
    loudness, own = 1.0, jax.random.fold_in(key, 6)
    for dim, shards_of in shards:
        steps = jnp.exp(jax.random.uniform(jax.random.fold_in(own, dim), (shards_of,), jnp.float32, low / len(shards), high / len(shards)))
        loudness = loudness * jnp.repeat(steps, shape[dim] // shards_of).reshape([-1 if axis == dim else 1 for axis in range(len(shape))])
    return loudness


def bell_draw(rng, dims, scale, bound, shards=(), kind=jnp.bfloat16):
    values = jax.random.normal(rng, dims, jnp.float32) * scale
    if len(shards) > 0:
        values = block_levels(rng, dims, shards, -0.22, 0.18) * values
    return jnp.clip(values, min=-bound, max=bound).astype(kind)


def setup_inputs(seed: int = 0) -> dict:
    streams_of = jax.random.split(jax.random.key(seed), 9)
    layer_input = bell_draw(streams_of[0], (TOKENS, D), 1.0, 6.0, ((0, 512),))
    output_grad = bell_draw(streams_of[1], (TOKENS, D), 1.0, 6.0, ((0, 512),))
    gate_weights = jnp.clip(0.1 + 0.9 * jax.random.uniform(streams_of[2], (TOKENS, 2), jnp.float32) ** block_levels(streams_of[2], (TOKENS, 2), ((0, 512),), -0.2, 0.2), 0.1, 1.0)
    expert_ids = draw_expert_ids(jax.random.fold_in(streams_of[8], 71), 0)
    slot_positions = draw_slot_positions(jax.random.fold_in(streams_of[8], 71), 0)
    keep_mask = draw_keep_mask(jax.random.fold_in(streams_of[8], 71), 0)
    weight_in = bell_draw(streams_of[6], (EXPERTS, D, FF), D ** -0.5, 0.25, ((0, 32), (2, 16)))
    weight_out = bell_draw(streams_of[7], (EXPERTS, FF, D), FF ** -0.5, 0.078125, ((0, 32), (1, 16)))
    return dict(layer_input=layer_input, output_grad=output_grad, gate_weights=gate_weights, expert_ids=expert_ids, slot_positions=slot_positions, keep_mask=keep_mask, weight_in=weight_in, weight_out=weight_out)


root_coef = 0.7978845608028654
cube_coef = 0.044715


def gelu_value(preact):
    inner_arg = root_coef * (preact + cube_coef * preact * preact * preact)
    return 0.5 * preact * (1.0 + jnp.tanh(inner_arg))


def gelu_slope(preact):
    inner_arg = root_coef * (preact + cube_coef * preact * preact * preact)
    tanh_value = jnp.tanh(inner_arg)
    return 0.5 * (1.0 + tanh_value) + 0.5 * preact * (1.0 - tanh_value * tanh_value) * root_coef * (1.0 + 3.0 * cube_coef * preact * preact)


def expert_backward(operands):
    rows_in, rows_cot, weight_first, weight_second = operands
    preact = jnp.dot(rows_in, weight_first, preferred_element_type=jnp.float32)
    hidden = gelu_value(preact).astype(jnp.bfloat16)
    backprop = jnp.dot(rows_cot, weight_second.T, preferred_element_type=jnp.float32)
    grad_pre = (gelu_slope(preact) * backprop).astype(jnp.bfloat16)
    grad_first = jnp.dot(rows_in.T, grad_pre, preferred_element_type=jnp.float32).astype(jnp.bfloat16)
    grad_second = jnp.dot(hidden.T, rows_cot, preferred_element_type=jnp.float32).astype(jnp.bfloat16)
    row_total = rows_in.shape[0]
    split_pre = grad_pre.astype(jnp.float32).reshape(row_total, N_DP, FF // N_DP)
    split_weight = weight_first.astype(jnp.float32).reshape(D, N_DP, FF // N_DP)
    pieces = jnp.einsum("rqf,dqf->qrd", split_pre, split_weight).astype(jnp.bfloat16)
    pieces = lax.optimization_barrier(pieces)
    rows_grad = jnp.sum(pieces.astype(jnp.float32), axis=0).astype(jnp.bfloat16)
    return grad_first, grad_second, rows_grad


def reference(layer_input, output_grad, gate_weights, expert_ids, slot_positions, keep_mask, weight_in, weight_out):
    device_count = TOKENS // TOK_DEV
    slot_total = device_count * EXPERTS * CAP
    source = (jnp.arange(TOKENS, dtype=jnp.int32) // TOK_DEV)[:, None]
    flat_index = (source * (EXPERTS * CAP) + expert_ids * CAP + slot_positions).astype(jnp.int32).reshape(-1)
    keep_float = keep_mask.astype(jnp.float32)[:, :, None]
    spread_input = layer_input.astype(jnp.float32)[:, None, :] * keep_float
    scaled = (gate_weights[:, :, None] * output_grad.astype(jnp.float32)[:, None, :]).astype(jnp.bfloat16)
    scaled = lax.optimization_barrier(scaled)
    spread_cotan = scaled.astype(jnp.float32) * keep_float
    buffer_input = jnp.zeros((slot_total, D), jnp.float32).at[flat_index].add(spread_input.reshape(-1, D)).astype(jnp.bfloat16)
    buffer_cotan = jnp.zeros((slot_total, D), jnp.float32).at[flat_index].add(spread_cotan.reshape(-1, D)).astype(jnp.bfloat16)
    rows_in = buffer_input.reshape(device_count, EXPERTS, CAP, D).transpose(1, 0, 2, 3).reshape(EXPERTS, device_count * CAP, D)
    rows_cot = buffer_cotan.reshape(device_count, EXPERTS, CAP, D).transpose(1, 0, 2, 3).reshape(EXPERTS, device_count * CAP, D)
    grad_first, grad_second, rows_grad = lax.map(expert_backward, (rows_in, rows_cot, weight_in, weight_out))
    back_rows = rows_grad.reshape(EXPERTS, device_count, CAP, D).transpose(1, 0, 2, 3).reshape(slot_total, D)
    picked = back_rows[flat_index].astype(jnp.float32).reshape(TOKENS, 2, D) * keep_float
    input_grad = jnp.sum(picked, axis=1).astype(jnp.bfloat16)
    return (input_grad, grad_first, grad_second)
```

```python
import jax
import jax.numpy as jnp
from jax import lax
from jax.experimental import pallas as pl
from jax.experimental.pallas import tpu as pltpu
from jax.sharding import PartitionSpec as P

MESH = pl.DeviceIdType.MESH
ROOT_COEF = 0.7978845608028654
CUBE_COEF = 0.044715
N_EXP = 32
N_Y = 8
CAP = 6
ROWS = N_EXP * CAP
HALF = ROWS // 2
BF16 = jnp.bfloat16
F32 = jnp.float32


def dot(a, b, dims):
    return lax.dot_general(a, b, (dims, ((), ())), preferred_element_type=F32)


NN = ((1,), (0,))
NT = ((1,), (1,))
TN = ((0,), (0,))


def iota(shape, dim):
    return lax.broadcasted_iota(jnp.int32, shape, dim)


def column(row):
    n = row.shape[1]
    eye = iota((n, n), 0) == iota((n, n), 1)
    return jnp.sum(jnp.where(eye, jnp.broadcast_to(row, (n, n)), 0.0), axis=1, keepdims=True)


def kernel(
    x_ref, g_ref, gate_ref, eid_ref, slot_ref, keep_ref, win_ref, wout_ref,
    out_ref, owin_ref, owout_ref,
    send, recv, rows, part, wp, dw, dw_out, dw_in, gp, rs_out, rs_in, back_out, back_in,
    a2a_s, a2a_r, ag_s, ag_r, w_s, w_r, dw_s, dw_r, rs_s, rs_r, back_s, back_r,
):
    d = lax.axis_index("dp")
    e = lax.axis_index("expert")
    y = lax.rem(d, N_Y)
    base = d - y
    right = (base + lax.rem(y + 1, N_Y), e)
    left = (base + lax.rem(y + N_Y - 1, N_Y), e)
    mate = (lax.rem(d + N_Y, 2 * N_Y), e)
    side = (right, left)

    def remote(src, dst, ssem, rsem, device):
        return pltpu.make_async_remote_copy(
            src_ref=src, dst_ref=dst, send_sem=ssem, recv_sem=rsem,
            device_id=device, device_id_type=MESH,
        )

    barrier = pltpu.get_barrier_semaphore()

    def greet(k, c):
        pl.semaphore_signal(barrier, 1, device_id=(d, lax.rem(e + k, N_EXP)), device_id_type=MESH)
        return c

    lax.fori_loop(1, N_EXP, greet, 0)
    for device in (right, left, mate):
        pl.semaphore_signal(barrier, 1, device_id=device, device_id_type=MESH)

    tokens = x_ref.shape[0]
    eid = eid_ref[...].astype(F32)
    slot = slot_ref[...].astype(F32)
    kept = keep_ref[...] > 0
    target = jnp.where(kept, eid * 16.0 + slot, -100.0)
    blk = N_EXP * 16
    row_id = iota((blk, tokens), 0).astype(F32)
    hot_in = jnp.zeros((blk, tokens), F32)
    hots = []
    scaled = []
    grad = g_ref[...].astype(F32)
    for k in range(2):
        t = jnp.broadcast_to(target[k : k + 1], (blk, tokens))
        hot_in = hot_in + jnp.where(row_id == t, 1.0, 0.0)
        hots.append(jnp.where(row_id == t + 8.0, 1.0, 0.0).astype(BF16))
        scaled.append((column(gate_ref[k : k + 1]) * grad).astype(BF16))
    hot = jnp.concatenate([hot_in.astype(BF16)] + hots, axis=1)
    source = jnp.concatenate([x_ref[...]] + scaled, axis=0)
    send[...] = dot(hot, source, NN).astype(BF16).reshape(send.shape)
    recv[pl.ds(e, 1)] = send[pl.ds(e, 1)]
    dw[...] = jnp.zeros_like(dw)

    pl.semaphore_wait(barrier, N_EXP - 1 + 3)

    def a2a(k):
        t = lax.rem(e + k, N_EXP)
        return remote(send.at[t], recv.at[e], a2a_s.at[t], a2a_r.at[e], (d, t))

    def a2a_from(k):
        t = lax.rem(e + N_EXP - k, N_EXP)
        return remote(send.at[t], recv.at[t], a2a_s.at[t], a2a_r.at[t], (d, t))

    def a2a_start(k, c):
        a2a(k).start()
        return c

    def a2a_wait_recv(k, c):
        a2a_from(k).wait_recv()
        return c

    def a2a_wait_send(k, c):
        a2a(k).wait_send()
        return c

    lax.fori_loop(1, N_EXP, a2a_start, 0)
    weights = [
        remote(win_ref, wp.at[0], w_s.at[0], w_r.at[0], mate),
        remote(wout_ref, wp.at[1], w_s.at[1], w_r.at[1], mate),
    ]
    for copy in weights:
        copy.start()
    lax.fori_loop(1, N_EXP, a2a_wait_recv, 0)

    q = iota((ROWS, blk), 1)
    lane = jnp.bitwise_and(q, 7)
    want = jnp.where(lane < CAP, lax.shift_right_logical(q, 4) * CAP + lane, -1)
    which = jnp.bitwise_and(lax.shift_right_logical(q, 3), 1)
    at_row = iota((ROWS, blk), 0) == want
    arrived = recv[...].reshape(blk, -1)
    for s in range(2):
        close = jnp.where(at_row & (which == s), 1.0, 0.0).astype(BF16)
        rows[s, 0] = dot(close, arrived, NN).astype(BF16)

    def place(way, n):
        return 2 * n + way

    def gather(way, i, src_slot, dst_slot):
        s = lax.rem(i + way, 2)
        return remote(
            rows.at[s, src_slot], rows.at[s, dst_slot], ag_s.at[way, i], ag_r.at[way, i], side[way]
        )

    for i in range(2):
        for way in range(2):
            gather(way, i, 0, place(way, 1)).start()

    def core(b, half, wi, wo, gp_at):
        ri = rows[0, pl.ds(2 * b, 2)].reshape(2 * ROWS, -1)
        rc = rows[1, pl.ds(2 * b, 2)].reshape(2 * ROWS, -1)
        pre = dot(wi[...], ri, NT)
        bp = dot(wo[...], rc, NT)
        sq = pre * pre
        h = jnp.tanh(ROOT_COEF * (pre + CUBE_COEF * sq * pre))
        up = 0.5 * (1.0 + h)
        slope = up + 0.5 * pre * (1.0 - h * h) * ROOT_COEF * (1.0 + 3.0 * CUBE_COEF * sq)
        g = (slope * bp).astype(BF16)
        gp_at[...] = g
        dw[half, 0] += dot(g, ri, NN)
        dw[half, 1] += dot((pre * up).astype(BF16), rc, NN)

    def project(b, wi, gp_at, first):
        p = dot(gp_at[...], wi[...], TN).reshape(2, ROWS, -1)
        if first:
            part[pl.ds(2 * b, 2)] = p
        else:
            part[pl.ds(2 * b, 2)] += p

    def own_step(n, c):
        for j in range(2):
            i = 2 * (n - 1) + j
            for way in range(2):
                gather(way, i, 0, place(way, n)).wait_recv()

            def forward():
                for way in range(2):
                    dst = jnp.where(n == 3, 1, place(way, n + 1))
                    gather(way, i + 2, place(way, n), dst).start()

            if j == 0:
                forward()
            else:
                pl.when(n < 3)(forward)
        core(n, 0, win_ref, wout_ref, gp.at[0])
        project(n, win_ref, gp.at[0], True)
        return c

    lax.fori_loop(1, 4, own_step, 0)

    for copy in weights:
        copy.wait_recv()

    def mate_step(n, c):
        core(n, 1, wp.at[0], wp.at[1], gp.at[1])
        project(n, wp.at[0], gp.at[1], False)
        return c

    lax.fori_loop(1, 4, mate_step, 0)

    for way in range(2):
        gather(way, 6, place(way, 3), 1).wait_recv()
    core(0, 1, wp.at[0], wp.at[1], gp.at[1])
    dw_out[...] = dw[1].astype(BF16)
    deltas = [remote(dw_out.at[i], dw_in.at[i], dw_s.at[i], dw_r.at[i], mate) for i in range(2)]
    for copy in deltas:
        copy.start()
    core(0, 0, win_ref, wout_ref, gp.at[0])
    project(0, win_ref, gp.at[0], True)
    project(0, wp.at[0], gp.at[1], False)

    def ring(way, i):
        return remote(
            rs_out.at[way, i], rs_in.at[way, i], rs_s.at[way, i], rs_r.at[way, i], side[way]
        )

    def span(way, i):
        h = (i + way) % 2
        return pl.ds(h * HALF, HALF)

    for i in range(7):
        far = 4 - (i + 1) // 2
        for way in range(2):
            at = 1 if far == 4 else 2 * far + 1 - way
            value = part[at, span(way, i)]
            if i >= 2:
                ring(way, i - 2).wait_recv()
                value = value + rs_in[way, i - 2].astype(F32)
            rs_out[way, i] = value.astype(BF16)
            ring(way, i).start()

    spread_q = iota((N_EXP * 8, ROWS), 0)
    spread_lane = jnp.bitwise_and(spread_q, 7)
    spread_want = jnp.where(
        spread_lane < CAP, lax.shift_right_logical(spread_q, 3) * CAP + spread_lane, -1
    )
    spread = jnp.where(iota((N_EXP * 8, ROWS), 1) == spread_want, 1.0, 0.0).astype(BF16)
    pick = jnp.zeros((tokens, N_EXP * 8), F32)
    column_id = iota((tokens, N_EXP * 8), 1).astype(F32)
    for k in range(2):
        t = jnp.where(kept[k : k + 1], eid[k : k + 1] * 8.0 + slot[k : k + 1], -100.0)
        pick = pick + jnp.where(column_id == column(t), 1.0, 0.0)
    pick = pick.astype(BF16)

    for i in (5, 6):
        for way in range(2):
            ring(way, i).wait_recv()
    sums = []
    for h in range(2):
        value = part[0, pl.ds(h * HALF, HALF)]
        for way in range(2):
            i = 6 if (6 + way) % 2 == h else 5
            value = value + rs_in[way, i].astype(F32)
        sums.append(value.astype(BF16))
    total = jnp.concatenate(sums, axis=0)
    back_out[...] = dot(spread, total, NN).reshape(back_out.shape).astype(BF16)
    back_in[pl.ds(e, 1)] = back_out[pl.ds(e, 1)]

    def back(k):
        t = lax.rem(e + k, N_EXP)
        return remote(back_out.at[t], back_in.at[e], back_s.at[t], back_r.at[e], (d, t))

    def back_from(k):
        t = lax.rem(e + N_EXP - k, N_EXP)
        return remote(back_out.at[t], back_in.at[t], back_s.at[t], back_r.at[t], (d, t))

    def back_start(k, c):
        back(k).start()
        return c

    def back_wait_recv(k, c):
        back_from(k).wait_recv()
        return c

    def back_wait_send(k, c):
        back(k).wait_send()
        return c

    lax.fori_loop(1, N_EXP, back_start, 0)
    lax.fori_loop(1, N_EXP, a2a_wait_send, 0)
    for copy in weights:
        copy.wait_send()

    def gather_wait_send(i, c):
        for way in range(2):
            gather(way, i, 0, 1).wait_send()
        return c

    lax.fori_loop(0, 7, gather_wait_send, 0)
    for i in range(7):
        for way in range(2):
            ring(way, i).wait_send()
    lax.fori_loop(1, N_EXP, back_wait_recv, 0)
    returned = back_in[...].astype(F32).reshape(N_EXP * 8, -1).astype(BF16)
    out_ref[...] = dot(pick, returned, NN).astype(BF16)
    lax.fori_loop(1, N_EXP, back_wait_send, 0)

    for copy in deltas:
        copy.wait_recv()
    owin_ref[...] = (dw[0, 0] + dw_in[0].astype(F32)).astype(BF16)
    owout_ref[...] = (dw[0, 1] + dw_in[1].astype(F32)).astype(BF16)
    for copy in deltas:
        copy.wait_send()


def body(x, g, gate, eid, slot, keep, weight_in, weight_out):
    tokens, width = x.shape
    hidden = weight_in.shape[2]
    dma = pltpu.SemaphoreType.DMA
    vmem = pl.BlockSpec(memory_space=pltpu.VMEM)
    out, dwin, dwout = pl.pallas_call(
        kernel,
        out_shape=(
            jax.ShapeDtypeStruct((tokens, width), BF16),
            jax.ShapeDtypeStruct((hidden, width), BF16),
            jax.ShapeDtypeStruct((hidden, width), BF16),
        ),
        in_specs=[vmem] * 8,
        out_specs=(vmem, vmem, vmem),
        scratch_shapes=[
            pltpu.VMEM((N_EXP, 16, width), BF16),
            pltpu.VMEM((N_EXP, 16, width), BF16),
            pltpu.VMEM((2, N_Y, ROWS, width), BF16),
            pltpu.VMEM((N_Y, ROWS, width), F32),
            pltpu.VMEM((2, hidden, width), BF16),
            pltpu.VMEM((2, 2, hidden, width), F32),
            pltpu.VMEM((2, hidden, width), BF16),
            pltpu.VMEM((2, hidden, width), BF16),
            pltpu.VMEM((2, hidden, 2 * ROWS), BF16),
            pltpu.VMEM((2, 7, HALF, width), BF16),
            pltpu.VMEM((2, 7, HALF, width), BF16),
            pltpu.VMEM((N_EXP, 8, width), BF16),
            pltpu.VMEM((N_EXP, 8, width), BF16),
            dma((N_EXP,)), dma((N_EXP,)),
            dma((2, 7)), dma((2, 7)),
            dma((2,)), dma((2,)),
            dma((2,)), dma((2,)),
            dma((2, 7)), dma((2, 7)),
            dma((N_EXP,)), dma((N_EXP,)),
        ],
        compiler_params=pltpu.CompilerParams(
            collective_id=0, has_side_effects=True, vmem_limit_bytes=56 * 1024 * 1024
        ),
        name="moe_backward",
    )(
        x, g, gate.T, eid.T, slot.T, keep.T,
        jnp.swapaxes(weight_in[0], 0, 1), weight_out[0],
    )
    return out, jnp.swapaxes(dwin, 0, 1)[None], dwout[None]


def solution(mesh):
    split = P(("dp", "expert"), None)
    w_in, w_out = P("expert", None, "dp"), P("expert", "dp", None)
    return jax.shard_map(
        body, mesh=mesh, in_specs=(split,) * 6 + (w_in, w_out),
        out_specs=(split, w_in, w_out), check_vma=False,
    )
```

```python
import jax
import jax.numpy as jnp
from jax import lax
from jax.experimental import pallas as pl
from jax.experimental.pallas import tpu as pltpu
from jax.sharding import PartitionSpec as P

MESH = pl.DeviceIdType.MESH
ROOT_COEF = 0.7978845608028654
CUBE_COEF = 0.044715
N_EXP = 32
N_Y = 8
CAP = 6
ROWS = N_EXP * CAP
HALF = ROWS // 2
BF16 = jnp.bfloat16
F32 = jnp.float32


def dot(a, b, dims):
    return lax.dot_general(a, b, (dims, ((), ())), preferred_element_type=F32)


NN = ((1,), (0,))
NT = ((1,), (1,))
TN = ((0,), (0,))


def iota(shape, dim):
    return lax.broadcasted_iota(jnp.int32, shape, dim)


def column(row):
    n = row.shape[1]
    eye = iota((n, n), 0) == iota((n, n), 1)
    return jnp.sum(jnp.where(eye, jnp.broadcast_to(row, (n, n)), 0.0), axis=1, keepdims=True)


def kernel(
    x_ref, g_ref, gate_ref, eid_ref, slot_ref, keep_ref, win_ref, wout_ref,
    out_ref, owin_ref, owout_ref,
    send, recv, rows, part, wp, dw, dw_out, dw_in, gp, rs_out, rs_in, back_out, back_in,
    a2a_s, a2a_r, ag_s, ag_r, w_s, w_r, dw_s, dw_r, rs_s, rs_r, back_s, back_r,
):
    d = lax.axis_index("dp")
    e = lax.axis_index("expert")
    y = lax.rem(d, N_Y)
    base = d - y
    right = (base + lax.rem(y + 1, N_Y), e)
    left = (base + lax.rem(y + N_Y - 1, N_Y), e)
    mate = (lax.rem(d + N_Y, 2 * N_Y), e)
    side = (right, left)

    def remote(src, dst, ssem, rsem, device):
        return pltpu.make_async_remote_copy(
            src_ref=src, dst_ref=dst, send_sem=ssem, recv_sem=rsem,
            device_id=device, device_id_type=MESH,
        )

    barrier = pltpu.get_barrier_semaphore()

    def greet(k, c):
        pl.semaphore_signal(barrier, 1, device_id=(d, lax.rem(e + k, N_EXP)), device_id_type=MESH)
        return c

    lax.fori_loop(1, N_EXP, greet, 0)
    for device in (right, left, mate):
        pl.semaphore_signal(barrier, 1, device_id=device, device_id_type=MESH)

    tokens = x_ref.shape[0]
    blk = N_EXP * 8
    eid = eid_ref[...].astype(F32)
    slot = slot_ref[...].astype(F32)
    target = jnp.where(keep_ref[...] > 0, eid * 8.0 + slot, -100.0)
    row_id = iota((blk, tokens), 0).astype(F32)
    hots = [
        jnp.where(row_id == jnp.broadcast_to(target[k : k + 1], (blk, tokens)), 1.0, 0.0)
        for k in range(2)
    ]
    send[0] = dot((hots[0] + hots[1]).astype(BF16), x_ref[...], NN).astype(BF16).reshape(send.shape[1:])
    grad = g_ref[...].astype(F32)
    scaled = [(column(gate_ref[k : k + 1]) * grad).astype(BF16) for k in range(2)]
    send[1] = dot(
        jnp.concatenate(hots, axis=1).astype(BF16), jnp.concatenate(scaled, axis=0), NN
    ).astype(BF16).reshape(send.shape[1:])
    for s in range(2):
        recv[s, pl.ds(e, 1)] = send[s, pl.ds(e, 1)]
    dw[...] = jnp.zeros_like(dw)

    pl.semaphore_wait(barrier, N_EXP - 1 + 3)

    def a2a(s, k):
        t = lax.rem(e + k, N_EXP)
        return remote(send.at[s, t], recv.at[s, e], a2a_s.at[s, t], a2a_r.at[s, e], (d, t))

    def a2a_from(s, k):
        t = lax.rem(e + N_EXP - k, N_EXP)
        return remote(send.at[s, t], recv.at[s, t], a2a_s.at[s, t], a2a_r.at[s, t], (d, t))

    def each_peer(act):
        def step(k, c):
            act(k)
            return c

        lax.fori_loop(1, N_EXP, step, 0)

    for s in range(2):
        each_peer(lambda k: a2a(s, k).start())

    q = iota((ROWS, blk), 1)
    lane = jnp.bitwise_and(q, 7)
    want = jnp.where(lane < CAP, lax.shift_right_logical(q, 3) * CAP + lane, -1)
    close = jnp.where(iota((ROWS, blk), 0) == want, 1.0, 0.0).astype(BF16)

    def gather(way, i):
        s, n = i % 2, i // 2
        sems = ag_s.at[way, i], ag_r.at[way, i], side[way]
        src = 0 if n == 0 else 2 * n + way
        if n == 3:
            cut = pl.ds(way * HALF, HALF)
            return remote(rows.at[s, src, cut], rows.at[s, 1, cut], *sems)
        return remote(rows.at[s, src], rows.at[s, 2 * n + 2 + way], *sems)

    weights = [
        remote(win_ref, wp.at[0], w_s.at[0], w_r.at[0], mate),
        remote(wout_ref, wp.at[1], w_s.at[1], w_r.at[1], mate),
    ]
    for s in range(2):
        each_peer(lambda k: a2a_from(s, k).wait_recv())
        arrived = recv[s].astype(F32).reshape(blk, -1).astype(BF16)
        rows[s, 0] = dot(close, arrived, NN).astype(BF16)
        for way in range(2):
            gather(way, s).start()
    for copy in weights:
        copy.start()

    def core(b, half, wi, wo, gp_at):
        ri = rows[0, pl.ds(2 * b, 2)].reshape(2 * ROWS, -1)
        rc = rows[1, pl.ds(2 * b, 2)].reshape(2 * ROWS, -1)
        pre = dot(wi[...], ri, NT)
        bp = dot(wo[...], rc, NT)
        sq = pre * pre
        h = jnp.tanh(ROOT_COEF * (pre + CUBE_COEF * sq * pre))
        up = 0.5 * (1.0 + h)
        slope = up + 0.5 * pre * (1.0 - h * h) * ROOT_COEF * (1.0 + 3.0 * CUBE_COEF * sq)
        g = (slope * bp).astype(BF16)
        gp_at[...] = g
        dw[half, 0] += dot(g, ri, NN)
        dw[half, 1] += dot((pre * up).astype(BF16), rc, NN)

    def project(b, wi, gp_at, first):
        p = dot(gp_at[...], wi[...], TN).reshape(2, ROWS, -1)
        if first:
            part[pl.ds(2 * b, 2)] = p
        else:
            part[pl.ds(2 * b, 2)] += p

    for n in range(1, 4):
        for i in (2 * n - 2, 2 * n - 1):
            for way in range(2):
                gather(way, i).wait_recv()
                gather(way, i + 2).start()
        core(n, 0, win_ref, wout_ref, gp.at[0])
        project(n, win_ref, gp.at[0], True)

    for copy in weights:
        copy.wait_recv()

    def mate_step(n, c):
        core(n, 1, wp.at[0], wp.at[1], gp.at[1])
        project(n, wp.at[0], gp.at[1], False)
        return c

    lax.fori_loop(1, 4, mate_step, 0)

    for i in (6, 7):
        for way in range(2):
            gather(way, i).wait_recv()
    core(0, 1, wp.at[0], wp.at[1], gp.at[1])
    dw_out[...] = dw[1].astype(BF16)
    deltas = [remote(dw_out.at[i], dw_in.at[i], dw_s.at[i], dw_r.at[i], mate) for i in range(2)]
    for copy in deltas:
        copy.start()
    core(0, 0, win_ref, wout_ref, gp.at[0])
    project(0, win_ref, gp.at[0], True)
    project(0, wp.at[0], gp.at[1], False)

    def ring(way, i):
        return remote(
            rs_out.at[way, i], rs_in.at[way, i], rs_s.at[way, i], rs_r.at[way, i], side[way]
        )

    def span(way, i):
        h = (i + way) % 2
        return pl.ds(h * HALF, HALF)

    for i in range(7):
        far = 4 - (i + 1) // 2
        for way in range(2):
            at = 1 if far == 4 else 2 * far + 1 - way
            value = part[at, span(way, i)]
            if i >= 2:
                ring(way, i - 2).wait_recv()
                value = value + rs_in[way, i - 2].astype(F32)
            rs_out[way, i] = value.astype(BF16)
            ring(way, i).start()

    spread_q = iota((blk, ROWS), 0)
    spread_lane = jnp.bitwise_and(spread_q, 7)
    spread_want = jnp.where(
        spread_lane < CAP, lax.shift_right_logical(spread_q, 3) * CAP + spread_lane, -1
    )
    spread = jnp.where(iota((blk, ROWS), 1) == spread_want, 1.0, 0.0).astype(BF16)
    column_id = iota((tokens, blk), 1).astype(F32)
    pick = jnp.zeros((tokens, blk), F32)
    for k in range(2):
        pick = pick + jnp.where(column_id == column(target[k : k + 1]), 1.0, 0.0)
    pick = pick.astype(BF16)

    for i in (5, 6):
        for way in range(2):
            ring(way, i).wait_recv()
    sums = []
    for h in range(2):
        value = part[0, pl.ds(h * HALF, HALF)]
        for way in range(2):
            i = 6 if (6 + way) % 2 == h else 5
            value = value + rs_in[way, i].astype(F32)
        sums.append(value.astype(BF16))
    total = jnp.concatenate(sums, axis=0)
    back_out[...] = dot(spread, total, NN).reshape(back_out.shape).astype(BF16)
    back_in[pl.ds(e, 1)] = back_out[pl.ds(e, 1)]

    def back(k):
        t = lax.rem(e + k, N_EXP)
        return remote(back_out.at[t], back_in.at[e], back_s.at[t], back_r.at[e], (d, t))

    def back_from(k):
        t = lax.rem(e + N_EXP - k, N_EXP)
        return remote(back_out.at[t], back_in.at[t], back_s.at[t], back_r.at[t], (d, t))

    each_peer(lambda k: back(k).start())
    for s in range(2):
        each_peer(lambda k: a2a(s, k).wait_send())
    for copy in weights:
        copy.wait_send()
    for way in range(2):
        for i in range(8):
            gather(way, i).wait_send()
        for i in range(7):
            ring(way, i).wait_send()
    each_peer(lambda k: back_from(k).wait_recv())
    returned = back_in[...].astype(F32).reshape(blk, -1).astype(BF16)
    out_ref[...] = dot(pick, returned, NN).astype(BF16)
    each_peer(lambda k: back(k).wait_send())

    for i, ref in ((0, owin_ref), (1, owout_ref)):
        deltas[i].wait_recv()
        ref[...] = (dw[0, i] + dw_in[i].astype(F32)).astype(BF16)
    for copy in deltas:
        copy.wait_send()


def body(x, g, gate, eid, slot, keep, weight_in, weight_out):
    tokens, width = x.shape
    hidden = weight_in.shape[2]
    dma = pltpu.SemaphoreType.DMA
    vmem = pl.BlockSpec(memory_space=pltpu.VMEM)
    out, dwin, dwout = pl.pallas_call(
        kernel,
        out_shape=(
            jax.ShapeDtypeStruct((tokens, width), BF16),
            jax.ShapeDtypeStruct((hidden, width), BF16),
            jax.ShapeDtypeStruct((hidden, width), BF16),
        ),
        in_specs=[vmem] * 8,
        out_specs=(vmem, vmem, vmem),
        scratch_shapes=[
            pltpu.VMEM((2, N_EXP, 8, width), BF16),
            pltpu.VMEM((2, N_EXP, 8, width), BF16),
            pltpu.VMEM((2, N_Y, ROWS, width), BF16),
            pltpu.VMEM((N_Y, ROWS, width), F32),
            pltpu.VMEM((2, hidden, width), BF16),
            pltpu.VMEM((2, 2, hidden, width), F32),
            pltpu.VMEM((2, hidden, width), BF16),
            pltpu.VMEM((2, hidden, width), BF16),
            pltpu.VMEM((2, hidden, 2 * ROWS), BF16),
            pltpu.VMEM((2, 7, HALF, width), BF16),
            pltpu.VMEM((2, 7, HALF, width), BF16),
            pltpu.VMEM((N_EXP, 8, width), BF16),
            pltpu.VMEM((N_EXP, 8, width), BF16),
            dma((2, N_EXP)), dma((2, N_EXP)),
            dma((2, 8)), dma((2, 8)),
            dma((2,)), dma((2,)),
            dma((2,)), dma((2,)),
            dma((2, 7)), dma((2, 7)),
            dma((N_EXP,)), dma((N_EXP,)),
        ],
        compiler_params=pltpu.CompilerParams(
            collective_id=0, has_side_effects=True, vmem_limit_bytes=56 * 1024 * 1024
        ),
        name="moe_backward",
    )(
        x, g, gate.T, eid.T, slot.T, keep.T,
        jnp.swapaxes(weight_in[0], 0, 1), weight_out[0],
    )
    return out, jnp.swapaxes(dwin, 0, 1)[None], dwout[None]


def solution(mesh):
    split = P(("dp", "expert"), None)
    w_in, w_out = P("expert", None, "dp"), P("expert", "dp", None)
    return jax.shard_map(
        body, mesh=mesh, in_specs=(split,) * 6 + (w_in, w_out),
        out_specs=(split, w_in, w_out), check_vma=False,
    )
```

```python
import jax
import jax.numpy as jnp
from jax import lax
from jax.experimental import pallas as pl
from jax.experimental.pallas import tpu as pltpu
from jax.sharding import PartitionSpec as P

MESH = pl.DeviceIdType.MESH
ROOT_COEF = 0.7978845608028654
CUBE_COEF = 0.044715
N_EXP = 32
N_Y = 8
CAP = 6
ROWS = N_EXP * CAP
HALF = ROWS // 2
BF16 = jnp.bfloat16
F32 = jnp.float32


def dot(a, b, dims):
    return lax.dot_general(a, b, (dims, ((), ())), preferred_element_type=F32)


NN = ((1,), (0,))
NT = ((1,), (1,))
TN = ((0,), (0,))


def iota(shape, dim):
    return lax.broadcasted_iota(jnp.int32, shape, dim)


def column(row):
    n = row.shape[1]
    eye = iota((n, n), 0) == iota((n, n), 1)
    return jnp.sum(jnp.where(eye, jnp.broadcast_to(row, (n, n)), 0.0), axis=1, keepdims=True)


def kernel(
    x_ref, g_ref, gate_ref, eid_ref, slot_ref, keep_ref, win_ref, wout_ref,
    out_ref, owin_ref, owout_ref,
    send, recv, rows, part, wp, dw, dw_out, dw_in, gp, rs_out, rs_in, back_out, back_in,
    a2a_s, a2a_r, ag_s, ag_r, w_s, w_r, dw_s, dw_r, rs_s, rs_r, back_s, back_r,
):
    d = lax.axis_index("dp")
    e = lax.axis_index("expert")
    y = lax.rem(d, N_Y)
    base = d - y
    right = (base + lax.rem(y + 1, N_Y), e)
    left = (base + lax.rem(y + N_Y - 1, N_Y), e)
    mate = (lax.rem(d + N_Y, 2 * N_Y), e)
    side = (right, left)

    def remote(src, dst, ssem, rsem, device):
        return pltpu.make_async_remote_copy(
            src_ref=src, dst_ref=dst, send_sem=ssem, recv_sem=rsem,
            device_id=device, device_id_type=MESH,
        )

    barrier = pltpu.get_barrier_semaphore()

    def greet(k, c):
        pl.semaphore_signal(barrier, 1, device_id=(d, lax.rem(e + k, N_EXP)), device_id_type=MESH)
        return c

    lax.fori_loop(1, N_EXP, greet, 0)
    for device in (right, left, mate):
        pl.semaphore_signal(barrier, 1, device_id=device, device_id_type=MESH)

    tokens = x_ref.shape[0]
    blk = N_EXP * 8
    eid = eid_ref[...].astype(F32)
    slot = slot_ref[...].astype(F32)
    target = jnp.where(keep_ref[...] > 0, eid * 8.0 + slot, -100.0)
    row_id = iota((blk, tokens), 0).astype(F32)
    hots = [
        jnp.where(row_id == jnp.broadcast_to(target[k : k + 1], (blk, tokens)), 1.0, 0.0)
        for k in range(2)
    ]
    send[0] = dot((hots[0] + hots[1]).astype(BF16), x_ref[...], NN).astype(BF16).reshape(send.shape[1:])
    grad = g_ref[...].astype(F32)
    scaled = [(column(gate_ref[k : k + 1]) * grad).astype(BF16) for k in range(2)]
    send[1] = dot(
        jnp.concatenate(hots, axis=1).astype(BF16), jnp.concatenate(scaled, axis=0), NN
    ).astype(BF16).reshape(send.shape[1:])
    for s in range(2):
        recv[s, pl.ds(e, 1)] = send[s, pl.ds(e, 1)]
    dw[...] = jnp.zeros_like(dw)

    pl.semaphore_wait(barrier, N_EXP - 1 + 3)

    def a2a(s, k):
        t = lax.rem(e + k, N_EXP)
        return remote(send.at[s, t], recv.at[s, e], a2a_s.at[s, t], a2a_r.at[s, e], (d, t))

    def a2a_from(s, k):
        t = lax.rem(e + N_EXP - k, N_EXP)
        return remote(send.at[s, t], recv.at[s, t], a2a_s.at[s, t], a2a_r.at[s, t], (d, t))

    def each_peer(act):
        def step(k, c):
            act(k)
            return c

        lax.fori_loop(1, N_EXP, step, 0)

    for s in range(2):
        each_peer(lambda k: a2a(s, k).start())

    q = iota((ROWS, blk), 1)
    lane = jnp.bitwise_and(q, 7)
    want = jnp.where(lane < CAP, lax.shift_right_logical(q, 3) * CAP + lane, -1)
    close = jnp.where(iota((ROWS, blk), 0) == want, 1.0, 0.0).astype(BF16)

    def gather(way, i):
        s, n = i % 2, i // 2
        sems = ag_s.at[way, i], ag_r.at[way, i], side[way]
        src = 0 if n == 0 else 2 * n + way
        if n == 3:
            cut = pl.ds(way * HALF, HALF)
            return remote(rows.at[s, src, cut], rows.at[s, 1, cut], *sems)
        return remote(rows.at[s, src], rows.at[s, 2 * n + 2 + way], *sems)

    mid = win_ref.shape[0] // 2
    cuts = [pl.ds(0, mid), pl.ds(mid, mid)]
    weights = [
        remote(ref.at[cut], wp.at[i, cut], w_s.at[h, i], w_r.at[h, i], mate)
        for h, cut in enumerate(cuts)
        for i, ref in enumerate((win_ref, wout_ref))
    ]
    deltas = [
        remote(dw_out.at[i, cut], dw_in.at[i, cut], dw_s.at[h, i], dw_r.at[h, i], mate)
        for h, cut in enumerate(cuts)
        for i in range(2)
    ]
    for s in range(2):
        each_peer(lambda k: a2a_from(s, k).wait_recv())
        arrived = recv[s].astype(F32).reshape(blk, -1).astype(BF16)
        rows[s, 0] = dot(close, arrived, NN).astype(BF16)
        for way in range(2):
            gather(way, s).start()
    for copy in weights:
        copy.start()

    def core(b, half, wi, wo, cut):
        ri = rows[0, pl.ds(2 * b, 2)].reshape(2 * ROWS, -1)
        rc = rows[1, pl.ds(2 * b, 2)].reshape(2 * ROWS, -1)
        pre = dot(wi[cut], ri, NT)
        bp = dot(wo[cut], rc, NT)
        sq = pre * pre
        h = jnp.tanh(ROOT_COEF * (pre + CUBE_COEF * sq * pre))
        up = 0.5 * (1.0 + h)
        slope = up + 0.5 * pre * (1.0 - h * h) * ROOT_COEF * (1.0 + 3.0 * CUBE_COEF * sq)
        g = (slope * bp).astype(BF16)
        gp[half, b, cut] = g
        dw[half, 0, cut] += dot(g, ri, NN)
        dw[half, 1, cut] += dot((pre * up).astype(BF16), rc, NN)

    def project(b, half, wi):
        p = dot(gp[half, b], wi[...], TN).reshape(2, ROWS, -1)
        if half == 0:
            part[pl.ds(2 * b, 2)] = p
        else:
            part[pl.ds(2 * b, 2)] += p

    whole = pl.ds(0, 2 * mid)
    for n in range(1, 4):
        for i in (2 * n - 2, 2 * n - 1):
            for way in range(2):
                gather(way, i).wait_recv()
                gather(way, i + 2).start()
        core(n, 0, win_ref, wout_ref, whole)
        project(n, 0, win_ref)

    for h, cut in enumerate(cuts):
        for copy in weights[2 * h : 2 * h + 2]:
            copy.wait_recv()

        def mate_step(b, c):
            core(b, 1, wp.at[0], wp.at[1], cut)
            return c

        if h == 0:
            lax.fori_loop(1, 4, mate_step, 0)
            for i in (6, 7):
                for way in range(2):
                    gather(way, i).wait_recv()
            mate_step(0, 0)
        else:
            lax.fori_loop(0, 4, mate_step, 0)
        for i in range(2):
            dw_out[i, cut] = dw[1, i, cut].astype(BF16)
            deltas[2 * h + i].start()
        if h == 0:
            core(0, 0, win_ref, wout_ref, whole)
            project(0, 0, win_ref)
    for b in (0, 3, 2, 1):
        project(b, 1, wp.at[0])

    def ring(way, i):
        return remote(
            rs_out.at[way, i], rs_in.at[way, i], rs_s.at[way, i], rs_r.at[way, i], side[way]
        )

    def span(way, i):
        h = (i + way) % 2
        return pl.ds(h * HALF, HALF)

    for i in range(7):
        far = 4 - (i + 1) // 2
        for way in range(2):
            at = 1 if far == 4 else 2 * far + 1 - way
            value = part[at, span(way, i)]
            if i >= 2:
                ring(way, i - 2).wait_recv()
                value = value + rs_in[way, i - 2].astype(F32)
            rs_out[way, i] = value.astype(BF16)
            ring(way, i).start()

    spread_q = iota((blk, ROWS), 0)
    spread_lane = jnp.bitwise_and(spread_q, 7)
    spread_want = jnp.where(
        spread_lane < CAP, lax.shift_right_logical(spread_q, 3) * CAP + spread_lane, -1
    )
    spread = jnp.where(iota((blk, ROWS), 1) == spread_want, 1.0, 0.0).astype(BF16)
    column_id = iota((tokens, blk), 1).astype(F32)
    pick = jnp.zeros((tokens, blk), F32)
    for k in range(2):
        pick = pick + jnp.where(column_id == column(target[k : k + 1]), 1.0, 0.0)
    pick = pick.astype(BF16)

    for i in (5, 6):
        for way in range(2):
            ring(way, i).wait_recv()
    sums = []
    for h in range(2):
        value = part[0, pl.ds(h * HALF, HALF)]
        for way in range(2):
            i = 6 if (6 + way) % 2 == h else 5
            value = value + rs_in[way, i].astype(F32)
        sums.append(value.astype(BF16))
    total = jnp.concatenate(sums, axis=0)
    back_out[...] = dot(spread, total, NN).reshape(back_out.shape).astype(BF16)
    back_in[pl.ds(e, 1)] = back_out[pl.ds(e, 1)]

    def back(k):
        t = lax.rem(e + k, N_EXP)
        return remote(back_out.at[t], back_in.at[e], back_s.at[t], back_r.at[e], (d, t))

    def back_from(k):
        t = lax.rem(e + N_EXP - k, N_EXP)
        return remote(back_out.at[t], back_in.at[t], back_s.at[t], back_r.at[t], (d, t))

    each_peer(lambda k: back(k).start())
    for s in range(2):
        each_peer(lambda k: a2a(s, k).wait_send())
    for copy in weights:
        copy.wait_send()
    for way in range(2):
        for i in range(8):
            gather(way, i).wait_send()
        for i in range(7):
            ring(way, i).wait_send()
    each_peer(lambda k: back_from(k).wait_recv())
    returned = back_in[...].astype(F32).reshape(blk, -1).astype(BF16)
    out_ref[...] = dot(pick, returned, NN).astype(BF16)
    each_peer(lambda k: back(k).wait_send())

    for h, cut in enumerate(cuts):
        for i, ref in enumerate((owin_ref, owout_ref)):
            deltas[2 * h + i].wait_recv()
            ref[cut] = (dw[0, i, cut] + dw_in[i, cut].astype(F32)).astype(BF16)
    for copy in deltas:
        copy.wait_send()


def hand_over(*refs):
    for src, dst in zip(refs[:3], refs[3:]):
        dst[...] = src[...]


def body(x, g, gate, eid, slot, keep, weight_in, weight_out):
    tokens, width = x.shape
    hidden = weight_in.shape[2]
    dma = pltpu.SemaphoreType.DMA
    vmem = pl.BlockSpec(memory_space=pltpu.VMEM)
    shapes = (
        jax.ShapeDtypeStruct((tokens, width), BF16),
        jax.ShapeDtypeStruct((hidden, width), BF16),
        jax.ShapeDtypeStruct((hidden, width), BF16),
    )
    results = pl.pallas_call(
        kernel,
        out_shape=shapes,
        in_specs=[vmem] * 8,
        out_specs=(vmem, vmem, vmem),
        scratch_shapes=[
            pltpu.VMEM((2, N_EXP, 8, width), BF16),
            pltpu.VMEM((2, N_EXP, 8, width), BF16),
            pltpu.VMEM((2, N_Y, ROWS, width), BF16),
            pltpu.VMEM((N_Y, ROWS, width), F32),
            pltpu.VMEM((2, hidden, width), BF16),
            pltpu.VMEM((2, 2, hidden, width), F32),
            pltpu.VMEM((2, hidden, width), BF16),
            pltpu.VMEM((2, hidden, width), BF16),
            pltpu.VMEM((2, N_Y // 2, hidden, 2 * ROWS), BF16),
            pltpu.VMEM((2, 7, HALF, width), BF16),
            pltpu.VMEM((2, 7, HALF, width), BF16),
            pltpu.VMEM((N_EXP, 8, width), BF16),
            pltpu.VMEM((N_EXP, 8, width), BF16),
            dma((2, N_EXP)), dma((2, N_EXP)),
            dma((2, 8)), dma((2, 8)),
            dma((2, 2)), dma((2, 2)),
            dma((2, 2)), dma((2, 2)),
            dma((2, 7)), dma((2, 7)),
            dma((N_EXP,)), dma((N_EXP,)),
        ],
        compiler_params=pltpu.CompilerParams(
            collective_id=0, has_side_effects=True, vmem_limit_bytes=56 * 1024 * 1024
        ),
        name="moe_backward",
    )(
        x, g, gate.T, eid.T, slot.T, keep.T,
        jnp.swapaxes(weight_in[0], 0, 1), weight_out[0],
    )
    out, dwin, dwout = pl.pallas_call(
        hand_over, out_shape=shapes, in_specs=[vmem] * 3, out_specs=(vmem,) * 3, name="hand_over"
    )(*results)
    return out, jnp.swapaxes(dwin, 0, 1)[None], dwout[None]


def solution(mesh):
    split = P(("dp", "expert"), None)
    w_in, w_out = P("expert", None, "dp"), P("expert", "dp", None)
    return jax.shard_map(
        body, mesh=mesh, in_specs=(split,) * 6 + (w_in, w_out),
        out_specs=(split, w_in, w_out), check_vma=False,
    )
```

```python
import jax
import jax.numpy as jnp
from jax import lax
from jax.experimental import pallas as pl
from jax.experimental.pallas import tpu as pltpu
from jax.sharding import PartitionSpec as P

MESH = pl.DeviceIdType.MESH
ROOT_COEF = 0.7978845608028654
CUBE_COEF = 0.044715
N_EXP = 32
N_Y = 8
CAP = 6
ROWS = N_EXP * CAP
HALF = ROWS // 2
LANES = 128
BLOCK = 32
GROUP = 8
BF16 = jnp.bfloat16
F32 = jnp.float32


def dot(a, b, dims):
    return lax.dot_general(a, b, (dims, ((), ())), preferred_element_type=F32)


NN = ((1,), (0,))
NT = ((1,), (1,))
TN = ((0,), (0,))


def iota(shape, dim):
    return lax.broadcasted_iota(jnp.int32, shape, dim)


def column(row):
    n = row.shape[1]
    eye = iota((n, n), 0) == iota((n, n), 1)
    return jnp.sum(jnp.where(eye, jnp.broadcast_to(row, (n, n)), 0.0), axis=1, keepdims=True)


def kernel(
    x_ref, g_ref, gate_ref, eid_ref, slot_ref, keep_ref, win_ref, wout_ref,
    out_ref, owin_ref, owout_ref,
    send, recv, rows, part, wp, dw, dw_out, dw_in, gp, rs_out, rs_in, back_out, back_in,
    a2a_s, a2a_r, ag_s, ag_r, w_s, w_r, dw_s, dw_r, rs_s, rs_r, back_s, back_r,
):
    d = lax.axis_index("dp")
    e = lax.axis_index("expert")
    y = lax.rem(d, N_Y)
    base = d - y
    right = (base + lax.rem(y + 1, N_Y), e)
    left = (base + lax.rem(y + N_Y - 1, N_Y), e)
    mate = (lax.rem(d + N_Y, 2 * N_Y), e)
    side = (right, left)

    def remote(src, dst, ssem, rsem, device):
        return pltpu.make_async_remote_copy(
            src_ref=src, dst_ref=dst, send_sem=ssem, recv_sem=rsem,
            device_id=device, device_id_type=MESH,
        )

    barrier = pltpu.get_barrier_semaphore()

    def greet(k, c):
        pl.semaphore_signal(barrier, 1, device_id=(d, lax.rem(e + k, N_EXP)), device_id_type=MESH)
        return c

    lax.fori_loop(1, N_EXP, greet, 0)
    for device in (right, left, mate):
        pl.semaphore_signal(barrier, 1, device_id=device, device_id_type=MESH)

    tokens, width = x_ref.shape
    tiles = width // LANES
    few = GROUP * CAP

    def packed_at(shape, dim):
        r = iota(shape, dim)
        inside = jnp.bitwise_and(r, BLOCK - 1)
        tile = lax.shift_right_logical(inside * 43, 8)
        at = tile * few + lax.shift_right_logical(r, 5) * CAP + inside - tile * CAP
        return jnp.where(inside < tiles * CAP, at, -1)

    wide = (GROUP * BLOCK, tiles * few)
    tall = (tiles * few, GROUP * BLOCK)
    spread = jnp.where(iota(wide, 1) == packed_at(wide, 0), 1.0, 0.0).astype(BF16)
    close = jnp.where(iota(tall, 0) == packed_at(tall, 1), 1.0, 0.0).astype(BF16)

    def pack(value, dst):
        for n in range(N_EXP // GROUP):
            some = value[n * few : (n + 1) * few]
            stack = jnp.concatenate(
                [some[:, t * LANES : (t + 1) * LANES] for t in range(tiles)], axis=0
            )
            out = dot(spread, stack, NN).astype(BF16)
            dst[pl.ds(n * GROUP, GROUP)] = out.reshape(GROUP, BLOCK, LANES)

    def unpack(src, n):
        out = dot(close, src[pl.ds(n * GROUP, GROUP)].reshape(GROUP * BLOCK, LANES), NN)
        out = out.astype(BF16)
        return jnp.concatenate([out[t * few : (t + 1) * few] for t in range(tiles)], axis=1)

    target = jnp.where(
        keep_ref[...] > 0, eid_ref[...].astype(F32) * float(CAP) + slot_ref[...].astype(F32), -100.0
    )
    row_id = iota((ROWS, tokens), 0).astype(F32)
    hots = [
        jnp.where(row_id == jnp.broadcast_to(target[k : k + 1], (ROWS, tokens)), 1.0, 0.0)
        for k in range(2)
    ]
    pack(dot((hots[0] + hots[1]).astype(BF16), x_ref[...], NN).astype(BF16), send.at[0])
    grad = g_ref[...].astype(F32)
    scaled = [(column(gate_ref[k : k + 1]) * grad).astype(BF16) for k in range(2)]
    pack(
        dot(
            jnp.concatenate(hots, axis=1).astype(BF16), jnp.concatenate(scaled, axis=0), NN
        ).astype(BF16),
        send.at[1],
    )
    for s in range(2):
        recv[s, pl.ds(e, 1)] = send[s, pl.ds(e, 1)]
    dw[...] = jnp.zeros_like(dw)

    pl.semaphore_wait(barrier, N_EXP - 1 + 3)

    def a2a(s, k):
        t = lax.rem(e + k, N_EXP)
        return remote(send.at[s, t], recv.at[s, e], a2a_s.at[s, t], a2a_r.at[s, e], (d, t))

    def a2a_from(s, k):
        t = lax.rem(e + N_EXP - k, N_EXP)
        return remote(send.at[s, t], recv.at[s, t], a2a_s.at[s, t], a2a_r.at[s, t], (d, t))

    def each_peer(act):
        def step(k, c):
            act(k)
            return c

        lax.fori_loop(1, N_EXP, step, 0)

    for s in range(2):
        each_peer(lambda k: a2a(s, k).start())

    def gather(way, i):
        s, n = i % 2, i // 2
        sems = ag_s.at[way, i], ag_r.at[way, i], side[way]
        src = 0 if n == 0 else 2 * n + way
        if n == 3:
            cut = pl.ds(way * HALF, HALF)
            return remote(rows.at[s, src, cut], rows.at[s, 1, cut], *sems)
        return remote(rows.at[s, src], rows.at[s, 2 * n + 2 + way], *sems)

    mid = win_ref.shape[0] // 2
    cuts = [pl.ds(0, mid), pl.ds(mid, mid)]
    weights = [
        remote(ref.at[cut], wp.at[i, cut], w_s.at[h, i], w_r.at[h, i], mate)
        for h, cut in enumerate(cuts)
        for i, ref in enumerate((win_ref, wout_ref))
    ]
    deltas = [
        remote(dw_out.at[i, cut], dw_in.at[i, cut], dw_s.at[h, i], dw_r.at[h, i], mate)
        for h, cut in enumerate(cuts)
        for i in range(2)
    ]
    for s in range(2):
        each_peer(lambda k: a2a_from(s, k).wait_recv())
        for n in range(N_EXP // GROUP):
            rows[s, 0, pl.ds(n * few, few)] = unpack(recv.at[s], n)
        for way in range(2):
            gather(way, s).start()
    for copy in weights:
        copy.start()

    def core(b, half, wi, wo, cut):
        ri = rows[0, pl.ds(2 * b, 2)].reshape(2 * ROWS, -1)
        rc = rows[1, pl.ds(2 * b, 2)].reshape(2 * ROWS, -1)
        pre = dot(wi[cut], ri, NT)
        bp = dot(wo[cut], rc, NT)
        sq = pre * pre
        h = jnp.tanh(ROOT_COEF * (pre + CUBE_COEF * sq * pre))
        up = 0.5 * (1.0 + h)
        slope = up + 0.5 * pre * (1.0 - h * h) * ROOT_COEF * (1.0 + 3.0 * CUBE_COEF * sq)
        g = (slope * bp).astype(BF16)
        gp[half, b, cut] = g
        dw[half, 0, cut] += dot(g, ri, NN)
        dw[half, 1, cut] += dot((pre * up).astype(BF16), rc, NN)

    def project(b, half, wi):
        p = dot(gp[half, b], wi[...], TN).reshape(2, ROWS, -1)
        if half == 0:
            part[pl.ds(2 * b, 2)] = p
        else:
            part[pl.ds(2 * b, 2)] += p

    whole = pl.ds(0, 2 * mid)
    for n in range(1, 4):
        for i in (2 * n - 2, 2 * n - 1):
            for way in range(2):
                gather(way, i).wait_recv()
                gather(way, i + 2).start()
        core(n, 0, win_ref, wout_ref, whole)
        project(n, 0, win_ref)

    for h, cut in enumerate(cuts):
        for copy in weights[2 * h : 2 * h + 2]:
            copy.wait_recv()

        def mate_step(b, c):
            core(b, 1, wp.at[0], wp.at[1], cut)
            return c

        if h == 0:
            lax.fori_loop(1, 4, mate_step, 0)
            for i in (6, 7):
                for way in range(2):
                    gather(way, i).wait_recv()
            mate_step(0, 0)
        else:
            lax.fori_loop(0, 4, mate_step, 0)
        for i in range(2):
            dw_out[i, cut] = dw[1, i, cut].astype(BF16)
            deltas[2 * h + i].start()
        if h == 0:
            core(0, 0, win_ref, wout_ref, whole)
            project(0, 0, win_ref)
    for b in (0, 3, 2, 1):
        project(b, 1, wp.at[0])

    def ring(way, i):
        return remote(
            rs_out.at[way, i], rs_in.at[way, i], rs_s.at[way, i], rs_r.at[way, i], side[way]
        )

    def span(way, i):
        h = (i + way) % 2
        return pl.ds(h * HALF, HALF)

    for i in range(7):
        far = 4 - (i + 1) // 2
        for way in range(2):
            at = 1 if far == 4 else 2 * far + 1 - way
            value = part[at, span(way, i)]
            if i >= 2:
                ring(way, i - 2).wait_recv()
                value = value + rs_in[way, i - 2].astype(F32)
            rs_out[way, i] = value.astype(BF16)
            ring(way, i).start()

    column_id = iota((tokens, ROWS), 1).astype(F32)
    pick = jnp.zeros((tokens, ROWS), F32)
    for k in range(2):
        pick = pick + jnp.where(column_id == column(target[k : k + 1]), 1.0, 0.0)
    pick = pick.astype(BF16)

    for i in (5, 6):
        for way in range(2):
            ring(way, i).wait_recv()
    sums = []
    for h in range(2):
        value = part[0, pl.ds(h * HALF, HALF)]
        for way in range(2):
            i = 6 if (6 + way) % 2 == h else 5
            value = value + rs_in[way, i].astype(F32)
        sums.append(value.astype(BF16))
    total = jnp.concatenate(sums, axis=0)
    pack(total, back_out)
    back_in[pl.ds(e, 1)] = back_out[pl.ds(e, 1)]

    def back(k):
        t = lax.rem(e + k, N_EXP)
        return remote(back_out.at[t], back_in.at[e], back_s.at[t], back_r.at[e], (d, t))

    def back_from(k):
        t = lax.rem(e + N_EXP - k, N_EXP)
        return remote(back_out.at[t], back_in.at[t], back_s.at[t], back_r.at[t], (d, t))

    each_peer(lambda k: back(k).start())
    for s in range(2):
        each_peer(lambda k: a2a(s, k).wait_send())
    for copy in weights:
        copy.wait_send()
    for way in range(2):
        for i in range(8):
            gather(way, i).wait_send()
        for i in range(7):
            ring(way, i).wait_send()
    each_peer(lambda k: back_from(k).wait_recv())
    returned = jnp.concatenate([unpack(back_in, n) for n in range(N_EXP // GROUP)], axis=0)
    out_ref[...] = dot(pick, returned, NN).astype(BF16)
    each_peer(lambda k: back(k).wait_send())

    for h, cut in enumerate(cuts):
        for i, ref in enumerate((owin_ref, owout_ref)):
            deltas[2 * h + i].wait_recv()
            ref[cut] = (dw[0, i, cut] + dw_in[i, cut].astype(F32)).astype(BF16)
    for copy in deltas:
        copy.wait_send()


def hand_over(*refs):
    for src, dst in zip(refs[:3], refs[3:]):
        dst[...] = src[...]


def body(x, g, gate, eid, slot, keep, weight_in, weight_out):
    tokens, width = x.shape
    hidden = weight_in.shape[2]
    dma = pltpu.SemaphoreType.DMA
    vmem = pl.BlockSpec(memory_space=pltpu.VMEM)
    shapes = (
        jax.ShapeDtypeStruct((tokens, width), BF16),
        jax.ShapeDtypeStruct((hidden, width), BF16),
        jax.ShapeDtypeStruct((hidden, width), BF16),
    )
    results = pl.pallas_call(
        kernel,
        out_shape=shapes,
        in_specs=[vmem] * 8,
        out_specs=(vmem, vmem, vmem),
        scratch_shapes=[
            pltpu.VMEM((2, N_EXP, BLOCK, LANES), BF16),
            pltpu.VMEM((2, N_EXP, BLOCK, LANES), BF16),
            pltpu.VMEM((2, N_Y, ROWS, width), BF16),
            pltpu.VMEM((N_Y, ROWS, width), F32),
            pltpu.VMEM((2, hidden, width), BF16),
            pltpu.VMEM((2, 2, hidden, width), F32),
            pltpu.VMEM((2, hidden, width), BF16),
            pltpu.VMEM((2, hidden, width), BF16),
            pltpu.VMEM((2, N_Y // 2, hidden, 2 * ROWS), BF16),
            pltpu.VMEM((2, 7, HALF, width), BF16),
            pltpu.VMEM((2, 7, HALF, width), BF16),
            pltpu.VMEM((N_EXP, BLOCK, LANES), BF16),
            pltpu.VMEM((N_EXP, BLOCK, LANES), BF16),
            dma((2, N_EXP)), dma((2, N_EXP)),
            dma((2, 8)), dma((2, 8)),
            dma((2, 2)), dma((2, 2)),
            dma((2, 2)), dma((2, 2)),
            dma((2, 7)), dma((2, 7)),
            dma((N_EXP,)), dma((N_EXP,)),
        ],
        compiler_params=pltpu.CompilerParams(
            collective_id=0, has_side_effects=True, vmem_limit_bytes=56 * 1024 * 1024
        ),
        name="moe_backward",
    )(
        x, g, gate.T, eid.T, slot.T, keep.T,
        jnp.swapaxes(weight_in[0], 0, 1), weight_out[0],
    )
    out, dwin, dwout = pl.pallas_call(
        hand_over, out_shape=shapes, in_specs=[vmem] * 3, out_specs=(vmem,) * 3, name="hand_over"
    )(*results)
    return out, jnp.swapaxes(dwin, 0, 1)[None], dwout[None]


def solution(mesh):
    split = P(("dp", "expert"), None)
    w_in, w_out = P("expert", None, "dp"), P("expert", "dp", None)
    return jax.shard_map(
        body, mesh=mesh, in_specs=(split,) * 6 + (w_in, w_out),
        out_specs=(split, w_in, w_out), check_vma=False,
    )
```

```python
import jax
import jax.numpy as jnp
from jax import lax
from jax.experimental import pallas as pl
from jax.experimental.pallas import tpu as pltpu
from jax.sharding import PartitionSpec as P

MESH = pl.DeviceIdType.MESH
ROOT_COEF = 0.7978845608028654
CUBE_COEF = 0.044715
N_EXP = 32
N_Y = 8
CAP = 6
ROWS = N_EXP * CAP
HALF = ROWS // 2
LANES = 128
BLOCK = 32
GROUP = 8
BF16 = jnp.bfloat16
F32 = jnp.float32


def dot(a, b, dims):
    return lax.dot_general(a, b, (dims, ((), ())), preferred_element_type=F32)


NN = ((1,), (0,))
NT = ((1,), (1,))
TN = ((0,), (0,))


def iota(shape, dim):
    return lax.broadcasted_iota(jnp.int32, shape, dim)


def column(row):
    n = row.shape[1]
    eye = iota((n, n), 0) == iota((n, n), 1)
    return jnp.sum(jnp.where(eye, jnp.broadcast_to(row, (n, n)), 0.0), axis=1, keepdims=True)


def kernel(
    x_ref, g_ref, gate_ref, eid_ref, slot_ref, keep_ref, win_ref, wout_ref,
    out_hbm, owin_hbm, owout_hbm,
    send, recv, rows, part, wp, dw, dw_out, dw_in, gp, rs_out, rs_in, back_out, back_in,
    out_ref, ow_ref, done,
    a2a_s, a2a_r, ag_s, ag_r, w_s, w_r, dw_s, dw_r, rs_s, rs_r, back_s, back_r,
):
    d = lax.axis_index("dp")
    e = lax.axis_index("expert")
    y = lax.rem(d, N_Y)
    base = d - y
    right = (base + lax.rem(y + 1, N_Y), e)
    left = (base + lax.rem(y + N_Y - 1, N_Y), e)
    mate = (lax.rem(d + N_Y, 2 * N_Y), e)
    side = (right, left)

    def remote(src, dst, ssem, rsem, device):
        return pltpu.make_async_remote_copy(
            src_ref=src, dst_ref=dst, send_sem=ssem, recv_sem=rsem,
            device_id=device, device_id_type=MESH,
        )

    barrier = pltpu.get_barrier_semaphore()

    def greet(k, c):
        pl.semaphore_signal(barrier, 1, device_id=(d, lax.rem(e + k, N_EXP)), device_id_type=MESH)
        return c

    lax.fori_loop(1, N_EXP, greet, 0)
    for device in (right, left, mate):
        pl.semaphore_signal(barrier, 1, device_id=device, device_id_type=MESH)

    tokens, width = x_ref.shape
    tiles = width // LANES
    few = GROUP * CAP

    def packed_at(shape, dim):
        r = iota(shape, dim)
        inside = jnp.bitwise_and(r, BLOCK - 1)
        tile = lax.shift_right_logical(inside * 43, 8)
        at = tile * few + lax.shift_right_logical(r, 5) * CAP + inside - tile * CAP
        return jnp.where(inside < tiles * CAP, at, -1)

    wide = (GROUP * BLOCK, tiles * few)
    tall = (tiles * few, GROUP * BLOCK)
    spread = jnp.where(iota(wide, 1) == packed_at(wide, 0), 1.0, 0.0).astype(BF16)
    close = jnp.where(iota(tall, 0) == packed_at(tall, 1), 1.0, 0.0).astype(BF16)

    def pack(value, dst):
        for n in range(N_EXP // GROUP):
            some = value[n * few : (n + 1) * few]
            stack = jnp.concatenate(
                [some[:, t * LANES : (t + 1) * LANES] for t in range(tiles)], axis=0
            )
            out = dot(spread, stack, NN).astype(BF16)
            dst[pl.ds(n * GROUP, GROUP)] = out.reshape(GROUP, BLOCK, LANES)

    def unpack(src, n):
        out = dot(close, src[pl.ds(n * GROUP, GROUP)].reshape(GROUP * BLOCK, LANES), NN)
        out = out.astype(BF16)
        return jnp.concatenate([out[t * few : (t + 1) * few] for t in range(tiles)], axis=1)

    target = jnp.where(
        keep_ref[...] > 0, eid_ref[...].astype(F32) * float(CAP) + slot_ref[...].astype(F32), -100.0
    )
    row_id = iota((ROWS, tokens), 0).astype(F32)
    hots = [
        jnp.where(row_id == jnp.broadcast_to(target[k : k + 1], (ROWS, tokens)), 1.0, 0.0)
        for k in range(2)
    ]
    pack(dot((hots[0] + hots[1]).astype(BF16), x_ref[...], NN).astype(BF16), send.at[0])
    grad = g_ref[...].astype(F32)
    scaled = [(column(gate_ref[k : k + 1]) * grad).astype(BF16) for k in range(2)]
    pack(
        dot(
            jnp.concatenate(hots, axis=1).astype(BF16), jnp.concatenate(scaled, axis=0), NN
        ).astype(BF16),
        send.at[1],
    )
    for s in range(2):
        recv[s, pl.ds(e, 1)] = send[s, pl.ds(e, 1)]
    dw[...] = jnp.zeros_like(dw)

    pl.semaphore_wait(barrier, N_EXP - 1 + 3)

    def a2a(s, k):
        t = lax.rem(e + k, N_EXP)
        return remote(send.at[s, t], recv.at[s, e], a2a_s.at[s, t], a2a_r.at[s, e], (d, t))

    def a2a_from(s, k):
        t = lax.rem(e + N_EXP - k, N_EXP)
        return remote(send.at[s, t], recv.at[s, t], a2a_s.at[s, t], a2a_r.at[s, t], (d, t))

    def each_peer(act):
        def step(k, c):
            act(k)
            return c

        lax.fori_loop(1, N_EXP, step, 0)

    for s in range(2):
        each_peer(lambda k: a2a(s, k).start())

    def gather(way, i):
        s, n = i % 2, i // 2
        sems = ag_s.at[way, i], ag_r.at[way, i], side[way]
        src = 0 if n == 0 else 2 * n + way
        if n == 3:
            cut = pl.ds(way * HALF, HALF)
            return remote(rows.at[s, src, cut], rows.at[s, 1, cut], *sems)
        return remote(rows.at[s, src], rows.at[s, 2 * n + 2 + way], *sems)

    mid = win_ref.shape[0] // 2
    cuts = [pl.ds(0, mid), pl.ds(mid, mid)]
    weights = [
        remote(ref.at[cut], wp.at[i, cut], w_s.at[h, i], w_r.at[h, i], mate)
        for h, cut in enumerate(cuts)
        for i, ref in enumerate((win_ref, wout_ref))
    ]
    deltas = [
        remote(dw_out.at[i, cut], dw_in.at[i, cut], dw_s.at[h, i], dw_r.at[h, i], mate)
        for h, cut in enumerate(cuts)
        for i in range(2)
    ]
    for s in range(2):
        each_peer(lambda k: a2a_from(s, k).wait_recv())
        for n in range(N_EXP // GROUP):
            rows[s, 0, pl.ds(n * few, few)] = unpack(recv.at[s], n)
        for way in range(2):
            gather(way, s).start()
    for copy in weights:
        copy.start()

    def core(b, half, wi, wo, cut):
        ri = rows[0, pl.ds(2 * b, 2)].reshape(2 * ROWS, -1)
        rc = rows[1, pl.ds(2 * b, 2)].reshape(2 * ROWS, -1)
        pre = dot(wi[cut], ri, NT)
        bp = dot(wo[cut], rc, NT)
        sq = pre * pre
        h = jnp.tanh(ROOT_COEF * (pre + CUBE_COEF * sq * pre))
        up = 0.5 * (1.0 + h)
        slope = up + 0.5 * pre * (1.0 - h * h) * ROOT_COEF * (1.0 + 3.0 * CUBE_COEF * sq)
        g = (slope * bp).astype(BF16)
        gp[half, b, cut] = g
        dw[half, 0, cut] += dot(g, ri, NN)
        dw[half, 1, cut] += dot((pre * up).astype(BF16), rc, NN)

    def project(b, half, wi):
        p = dot(gp[half, b], wi[...], TN).reshape(2, ROWS, -1)
        if half == 0:
            part[pl.ds(2 * b, 2)] = p
        else:
            part[pl.ds(2 * b, 2)] += p

    whole = pl.ds(0, 2 * mid)
    for n in range(1, 4):
        for i in (2 * n - 2, 2 * n - 1):
            for way in range(2):
                gather(way, i).wait_recv()
                gather(way, i + 2).start()
        core(n, 0, win_ref, wout_ref, whole)
        project(n, 0, win_ref)

    for h, cut in enumerate(cuts):
        for copy in weights[2 * h : 2 * h + 2]:
            copy.wait_recv()

        def mate_step(b, c):
            core(b, 1, wp.at[0], wp.at[1], cut)
            return c

        if h == 0:
            lax.fori_loop(1, 4, mate_step, 0)
            for i in (6, 7):
                for way in range(2):
                    gather(way, i).wait_recv()
            mate_step(0, 0)
        else:
            lax.fori_loop(0, 4, mate_step, 0)
        for i in range(2):
            dw_out[i, cut] = dw[1, i, cut].astype(BF16)
            deltas[2 * h + i].start()
        if h == 0:
            core(0, 0, win_ref, wout_ref, whole)
            project(0, 0, win_ref)
    for b in (0, 3, 2, 1):
        project(b, 1, wp.at[0])

    def ring(way, i):
        return remote(
            rs_out.at[way, i], rs_in.at[way, i], rs_s.at[way, i], rs_r.at[way, i], side[way]
        )

    def span(way, i):
        h = (i + way) % 2
        return pl.ds(h * HALF, HALF)

    for i in range(7):
        far = 4 - (i + 1) // 2
        for way in range(2):
            at = 1 if far == 4 else 2 * far + 1 - way
            value = part[at, span(way, i)]
            if i >= 2:
                ring(way, i - 2).wait_recv()
                value = value + rs_in[way, i - 2].astype(F32)
            rs_out[way, i] = value.astype(BF16)
            ring(way, i).start()

    column_id = iota((tokens, ROWS), 1).astype(F32)
    pick = jnp.zeros((tokens, ROWS), F32)
    for k in range(2):
        pick = pick + jnp.where(column_id == column(target[k : k + 1]), 1.0, 0.0)
    pick = pick.astype(BF16)

    for i in (5, 6):
        for way in range(2):
            ring(way, i).wait_recv()
    sums = []
    for h in range(2):
        value = part[0, pl.ds(h * HALF, HALF)]
        for way in range(2):
            i = 6 if (6 + way) % 2 == h else 5
            value = value + rs_in[way, i].astype(F32)
        sums.append(value.astype(BF16))
    total = jnp.concatenate(sums, axis=0)
    pack(total, back_out)
    back_in[pl.ds(e, 1)] = back_out[pl.ds(e, 1)]

    def back(k):
        t = lax.rem(e + k, N_EXP)
        return remote(back_out.at[t], back_in.at[e], back_s.at[t], back_r.at[e], (d, t))

    def back_from(k):
        t = lax.rem(e + N_EXP - k, N_EXP)
        return remote(back_out.at[t], back_in.at[t], back_s.at[t], back_r.at[t], (d, t))

    each_peer(lambda k: back(k).start())
    for s in range(2):
        each_peer(lambda k: a2a(s, k).wait_send())
    for copy in weights:
        copy.wait_send()
    for way in range(2):
        for i in range(8):
            gather(way, i).wait_send()
        for i in range(7):
            ring(way, i).wait_send()
    each_peer(lambda k: back_from(k).wait_recv())
    returned = jnp.concatenate([unpack(back_in, n) for n in range(N_EXP // GROUP)], axis=0)
    out_ref[...] = dot(pick, returned, NN).astype(BF16)
    results = [pltpu.make_async_copy(out_ref, out_hbm, done.at[0])]
    results[0].start()
    each_peer(lambda k: back(k).wait_send())

    for h, cut in enumerate(cuts):
        for i, ref in enumerate((owin_hbm, owout_hbm)):
            deltas[2 * h + i].wait_recv()
            ow_ref[i, cut] = (dw[0, i, cut] + dw_in[i, cut].astype(F32)).astype(BF16)
            results.append(
                pltpu.make_async_copy(ow_ref.at[i, cut], ref.at[cut], done.at[1 + 2 * h + i])
            )
            results[-1].start()
    for copy in deltas:
        copy.wait_send()
    for copy in results:
        copy.wait()


def hand_over(*refs):
    for src, dst in zip(refs[:3], refs[3:]):
        dst[...] = src[...]


def body(x, g, gate, eid, slot, keep, weight_in, weight_out):
    tokens, width = x.shape
    hidden = weight_in.shape[2]
    dma = pltpu.SemaphoreType.DMA
    vmem = pl.BlockSpec(memory_space=pltpu.VMEM)
    shapes = (
        jax.ShapeDtypeStruct((tokens, width), BF16),
        jax.ShapeDtypeStruct((hidden, width), BF16),
        jax.ShapeDtypeStruct((hidden, width), BF16),
    )
    results = pl.pallas_call(
        kernel,
        out_shape=shapes,
        in_specs=[vmem] * 8,
        out_specs=(pl.BlockSpec(memory_space=pl.ANY),) * 3,
        scratch_shapes=[
            pltpu.VMEM((2, N_EXP, BLOCK, LANES), BF16),
            pltpu.VMEM((2, N_EXP, BLOCK, LANES), BF16),
            pltpu.VMEM((2, N_Y, ROWS, width), BF16),
            pltpu.VMEM((N_Y, ROWS, width), F32),
            pltpu.VMEM((2, hidden, width), BF16),
            pltpu.VMEM((2, 2, hidden, width), F32),
            pltpu.VMEM((2, hidden, width), BF16),
            pltpu.VMEM((2, hidden, width), BF16),
            pltpu.VMEM((2, N_Y // 2, hidden, 2 * ROWS), BF16),
            pltpu.VMEM((2, 7, HALF, width), BF16),
            pltpu.VMEM((2, 7, HALF, width), BF16),
            pltpu.VMEM((N_EXP, BLOCK, LANES), BF16),
            pltpu.VMEM((N_EXP, BLOCK, LANES), BF16),
            pltpu.VMEM((tokens, width), BF16),
            pltpu.VMEM((2, hidden, width), BF16),
            dma((5,)),
            dma((2, N_EXP)), dma((2, N_EXP)),
            dma((2, 8)), dma((2, 8)),
            dma((2, 2)), dma((2, 2)),
            dma((2, 2)), dma((2, 2)),
            dma((2, 7)), dma((2, 7)),
            dma((N_EXP,)), dma((N_EXP,)),
        ],
        compiler_params=pltpu.CompilerParams(
            collective_id=0, has_side_effects=True, vmem_limit_bytes=36 * 1024 * 1024
        ),
        name="moe_backward",
    )(
        x, g, gate.T, eid.T, slot.T, keep.T,
        jnp.swapaxes(weight_in[0], 0, 1), weight_out[0],
    )
    out, dwin, dwout = results
    return out, jnp.swapaxes(dwin, 0, 1)[None], dwout[None]


def solution(mesh):
    split = P(("dp", "expert"), None)
    w_in, w_out = P("expert", None, "dp"), P("expert", "dp", None)
    return jax.shard_map(
        body, mesh=mesh, in_specs=(split,) * 6 + (w_in, w_out),
        out_specs=(split, w_in, w_out), check_vma=False,
    )
```

```python
import jax
import jax.numpy as jnp
from jax import lax
from jax.experimental import pallas as pl
from jax.experimental.pallas import tpu as pltpu
from jax.sharding import PartitionSpec as P

MESH = pl.DeviceIdType.MESH
ROOT_COEF = 0.7978845608028654
CUBE_COEF = 0.044715
N_EXP = 32
N_Y = 8
CAP = 6
ROWS = N_EXP * CAP
HALF = ROWS // 2
LANES = 128
BLOCK = 32
GROUP = 8
BF16 = jnp.bfloat16
F32 = jnp.float32


def dot(a, b, dims):
    return lax.dot_general(a, b, (dims, ((), ())), preferred_element_type=F32)


NN = ((1,), (0,))
NT = ((1,), (1,))
TN = ((0,), (0,))


def iota(shape, dim):
    return lax.broadcasted_iota(jnp.int32, shape, dim)


def column(row):
    n = row.shape[1]
    eye = iota((n, n), 0) == iota((n, n), 1)
    return jnp.sum(jnp.where(eye, jnp.broadcast_to(row, (n, n)), 0.0), axis=1, keepdims=True)


def kernel(
    x_hbm, g_hbm, gate_hbm, eid_hbm, slot_hbm, keep_hbm, win_hbm, wout_hbm,
    out_hbm, owin_hbm, owout_hbm,
    x_ref, g_ref, gate_ref, eid_ref, slot_ref, keep_ref, win_ref, wout_ref, load,
    send, recv, rows, part, wp, dw, dw_out, dw_in, gp, rs_out, rs_in, back_out, back_in,
    out_ref, ow_ref, done,
    a2a_s, a2a_r, ag_s, ag_r, w_s, w_r, dw_s, dw_r, rs_s, rs_r, back_s, back_r,
):
    d = lax.axis_index("dp")
    e = lax.axis_index("expert")
    y = lax.rem(d, N_Y)
    base = d - y
    right = (base + lax.rem(y + 1, N_Y), e)
    left = (base + lax.rem(y + N_Y - 1, N_Y), e)
    mate = (lax.rem(d + N_Y, 2 * N_Y), e)
    side = (right, left)

    def remote(src, dst, ssem, rsem, device):
        return pltpu.make_async_remote_copy(
            src_ref=src, dst_ref=dst, send_sem=ssem, recv_sem=rsem,
            device_id=device, device_id_type=MESH,
        )

    barrier = pltpu.get_barrier_semaphore()

    def greet(k, c):
        pl.semaphore_signal(barrier, 1, device_id=(d, lax.rem(e + k, N_EXP)), device_id_type=MESH)
        return c

    lax.fori_loop(1, N_EXP, greet, 0)
    for device in (right, left, mate):
        pl.semaphore_signal(barrier, 1, device_id=device, device_id_type=MESH)

    sources = (x_hbm, g_hbm, gate_hbm, eid_hbm, slot_hbm, keep_hbm, win_hbm, wout_hbm)
    places = (x_ref, g_ref, gate_ref, eid_ref, slot_ref, keep_ref, win_ref, wout_ref)
    loads = [
        pltpu.make_async_copy(source, place, load.at[i])
        for i, (source, place) in enumerate(zip(sources, places))
    ]
    for copy in loads:
        copy.start()

    tokens, width = x_ref.shape
    tiles = width // LANES
    few = GROUP * CAP

    def packed_at(shape, dim):
        r = iota(shape, dim)
        inside = jnp.bitwise_and(r, BLOCK - 1)
        tile = lax.shift_right_logical(inside * 43, 8)
        at = tile * few + lax.shift_right_logical(r, 5) * CAP + inside - tile * CAP
        return jnp.where(inside < tiles * CAP, at, -1)

    wide = (GROUP * BLOCK, tiles * few)
    tall = (tiles * few, GROUP * BLOCK)
    spread = jnp.where(iota(wide, 1) == packed_at(wide, 0), 1.0, 0.0).astype(BF16)
    close = jnp.where(iota(tall, 0) == packed_at(tall, 1), 1.0, 0.0).astype(BF16)

    def pack(value, dst):
        for n in range(N_EXP // GROUP):
            some = value[n * few : (n + 1) * few]
            stack = jnp.concatenate(
                [some[:, t * LANES : (t + 1) * LANES] for t in range(tiles)], axis=0
            )
            out = dot(spread, stack, NN).astype(BF16)
            dst[pl.ds(n * GROUP, GROUP)] = out.reshape(GROUP, BLOCK, LANES)

    def unpack(src, n):
        out = dot(close, src[pl.ds(n * GROUP, GROUP)].reshape(GROUP * BLOCK, LANES), NN)
        out = out.astype(BF16)
        return jnp.concatenate([out[t * few : (t + 1) * few] for t in range(tiles)], axis=1)

    for copy in loads:
        copy.wait()
    target = jnp.where(
        keep_ref[...] > 0, eid_ref[...].astype(F32) * float(CAP) + slot_ref[...].astype(F32), -100.0
    )
    row_id = iota((ROWS, tokens), 0).astype(F32)
    hots = [
        jnp.where(row_id == jnp.broadcast_to(target[k : k + 1], (ROWS, tokens)), 1.0, 0.0)
        for k in range(2)
    ]
    pack(dot((hots[0] + hots[1]).astype(BF16), x_ref[...], NN).astype(BF16), send.at[0])
    grad = g_ref[...].astype(F32)
    scaled = [(column(gate_ref[k : k + 1]) * grad).astype(BF16) for k in range(2)]
    pack(
        dot(
            jnp.concatenate(hots, axis=1).astype(BF16), jnp.concatenate(scaled, axis=0), NN
        ).astype(BF16),
        send.at[1],
    )
    for s in range(2):
        recv[s, pl.ds(e, 1)] = send[s, pl.ds(e, 1)]
    dw[...] = jnp.zeros_like(dw)

    pl.semaphore_wait(barrier, N_EXP - 1 + 3)

    def a2a(s, k):
        t = lax.rem(e + k, N_EXP)
        return remote(send.at[s, t], recv.at[s, e], a2a_s.at[s, t], a2a_r.at[s, e], (d, t))

    def a2a_from(s, k):
        t = lax.rem(e + N_EXP - k, N_EXP)
        return remote(send.at[s, t], recv.at[s, t], a2a_s.at[s, t], a2a_r.at[s, t], (d, t))

    def each_peer(act):
        def step(k, c):
            act(k)
            return c

        lax.fori_loop(1, N_EXP, step, 0)

    for s in range(2):
        each_peer(lambda k: a2a(s, k).start())

    def gather(way, i):
        s, n = i % 2, i // 2
        sems = ag_s.at[way, i], ag_r.at[way, i], side[way]
        src = 0 if n == 0 else 2 * n + way
        if n == 3:
            cut = pl.ds(way * HALF, HALF)
            return remote(rows.at[s, src, cut], rows.at[s, 1, cut], *sems)
        return remote(rows.at[s, src], rows.at[s, 2 * n + 2 + way], *sems)

    mid = win_ref.shape[0] // 2
    cuts = [pl.ds(0, mid), pl.ds(mid, mid)]
    weights = [
        remote(ref.at[cut], wp.at[i, cut], w_s.at[h, i], w_r.at[h, i], mate)
        for h, cut in enumerate(cuts)
        for i, ref in enumerate((win_ref, wout_ref))
    ]
    deltas = [
        remote(dw_out.at[i, cut], dw_in.at[i, cut], dw_s.at[h, i], dw_r.at[h, i], mate)
        for h, cut in enumerate(cuts)
        for i in range(2)
    ]
    for s in range(2):
        each_peer(lambda k: a2a_from(s, k).wait_recv())
        for n in range(N_EXP // GROUP):
            rows[s, 0, pl.ds(n * few, few)] = unpack(recv.at[s], n)
        for way in range(2):
            gather(way, s).start()
    for copy in weights:
        copy.start()

    def core(b, half, wi, wo, cut):
        ri = rows[0, pl.ds(2 * b, 2)].reshape(2 * ROWS, -1)
        rc = rows[1, pl.ds(2 * b, 2)].reshape(2 * ROWS, -1)
        pre = dot(wi[cut], ri, NT)
        bp = dot(wo[cut], rc, NT)
        sq = pre * pre
        h = jnp.tanh(ROOT_COEF * (pre + CUBE_COEF * sq * pre))
        up = 0.5 * (1.0 + h)
        slope = up + 0.5 * pre * (1.0 - h * h) * ROOT_COEF * (1.0 + 3.0 * CUBE_COEF * sq)
        g = (slope * bp).astype(BF16)
        gp[half, b, cut] = g
        dw[half, 0, cut] += dot(g, ri, NN)
        dw[half, 1, cut] += dot((pre * up).astype(BF16), rc, NN)

    def project(b, half, wi):
        p = dot(gp[half, b], wi[...], TN).reshape(2, ROWS, -1)
        if half == 0:
            part[pl.ds(2 * b, 2)] = p
        else:
            part[pl.ds(2 * b, 2)] += p

    whole = pl.ds(0, 2 * mid)
    for n in range(1, 4):
        for i in (2 * n - 2, 2 * n - 1):
            for way in range(2):
                gather(way, i).wait_recv()
                gather(way, i + 2).start()
        core(n, 0, win_ref, wout_ref, whole)
        project(n, 0, win_ref)

    for h, cut in enumerate(cuts):
        for copy in weights[2 * h : 2 * h + 2]:
            copy.wait_recv()

        def mate_step(b, c):
            core(b, 1, wp.at[0], wp.at[1], cut)
            return c

        if h == 0:
            lax.fori_loop(1, 4, mate_step, 0)
            for i in (6, 7):
                for way in range(2):
                    gather(way, i).wait_recv()
            mate_step(0, 0)
        else:
            lax.fori_loop(0, 4, mate_step, 0)
        for i in range(2):
            dw_out[i, cut] = dw[1, i, cut].astype(BF16)
            deltas[2 * h + i].start()
        if h == 0:
            core(0, 0, win_ref, wout_ref, whole)
            project(0, 0, win_ref)
    for b in (0, 3, 2, 1):
        project(b, 1, wp.at[0])

    def ring(way, i):
        return remote(
            rs_out.at[way, i], rs_in.at[way, i], rs_s.at[way, i], rs_r.at[way, i], side[way]
        )

    def span(way, i):
        h = (i + way) % 2
        return pl.ds(h * HALF, HALF)

    for i in range(7):
        far = 4 - (i + 1) // 2
        for way in range(2):
            at = 1 if far == 4 else 2 * far + 1 - way
            value = part[at, span(way, i)]
            if i >= 2:
                ring(way, i - 2).wait_recv()
                value = value + rs_in[way, i - 2].astype(F32)
            rs_out[way, i] = value.astype(BF16)
            ring(way, i).start()

    column_id = iota((tokens, ROWS), 1).astype(F32)
    pick = jnp.zeros((tokens, ROWS), F32)
    for k in range(2):
        pick = pick + jnp.where(column_id == column(target[k : k + 1]), 1.0, 0.0)
    pick = pick.astype(BF16)

    for i in (5, 6):
        for way in range(2):
            ring(way, i).wait_recv()
    sums = []
    for h in range(2):
        value = part[0, pl.ds(h * HALF, HALF)]
        for way in range(2):
            i = 6 if (6 + way) % 2 == h else 5
            value = value + rs_in[way, i].astype(F32)
        sums.append(value.astype(BF16))
    total = jnp.concatenate(sums, axis=0)
    pack(total, back_out)
    back_in[pl.ds(e, 1)] = back_out[pl.ds(e, 1)]

    def back(k):
        t = lax.rem(e + k, N_EXP)
        return remote(back_out.at[t], back_in.at[e], back_s.at[t], back_r.at[e], (d, t))

    def back_from(k):
        t = lax.rem(e + N_EXP - k, N_EXP)
        return remote(back_out.at[t], back_in.at[t], back_s.at[t], back_r.at[t], (d, t))

    each_peer(lambda k: back(k).start())
    for s in range(2):
        each_peer(lambda k: a2a(s, k).wait_send())
    for copy in weights:
        copy.wait_send()
    for way in range(2):
        for i in range(8):
            gather(way, i).wait_send()
        for i in range(7):
            ring(way, i).wait_send()
    each_peer(lambda k: back_from(k).wait_recv())
    returned = jnp.concatenate([unpack(back_in, n) for n in range(N_EXP // GROUP)], axis=0)
    out_ref[...] = dot(pick, returned, NN).astype(BF16)
    results = [pltpu.make_async_copy(out_ref, out_hbm, done.at[0])]
    results[0].start()
    each_peer(lambda k: back(k).wait_send())

    for h, cut in enumerate(cuts):
        for i, ref in enumerate((owin_hbm, owout_hbm)):
            deltas[2 * h + i].wait_recv()
            ow_ref[i, cut] = (dw[0, i, cut] + dw_in[i, cut].astype(F32)).astype(BF16)
            results.append(
                pltpu.make_async_copy(ow_ref.at[i, cut], ref.at[cut], done.at[1 + 2 * h + i])
            )
            results[-1].start()
    for copy in deltas:
        copy.wait_send()
    for copy in results:
        copy.wait()


def hand_over(*refs):
    for src, dst in zip(refs[:3], refs[3:]):
        dst[...] = src[...]


def body(x, g, gate, eid, slot, keep, weight_in, weight_out):
    tokens, width = x.shape
    hidden = weight_in.shape[2]
    dma = pltpu.SemaphoreType.DMA
    vmem = pl.BlockSpec(memory_space=pltpu.VMEM)
    shapes = (
        jax.ShapeDtypeStruct((tokens, width), BF16),
        jax.ShapeDtypeStruct((hidden, width), BF16),
        jax.ShapeDtypeStruct((hidden, width), BF16),
    )
    results = pl.pallas_call(
        kernel,
        out_shape=shapes,
        in_specs=[pl.BlockSpec(memory_space=pl.ANY)] * 8,
        out_specs=(pl.BlockSpec(memory_space=pl.ANY),) * 3,
        scratch_shapes=[
            pltpu.VMEM((tokens, width), BF16),
            pltpu.VMEM((tokens, width), BF16),
            pltpu.VMEM((2, tokens), F32),
            pltpu.VMEM((2, tokens), jnp.int32),
            pltpu.VMEM((2, tokens), jnp.int32),
            pltpu.VMEM((2, tokens), jnp.int32),
            pltpu.VMEM((hidden, width), BF16),
            pltpu.VMEM((hidden, width), BF16),
            dma((8,)),
            pltpu.VMEM((2, N_EXP, BLOCK, LANES), BF16),
            pltpu.VMEM((2, N_EXP, BLOCK, LANES), BF16),
            pltpu.VMEM((2, N_Y, ROWS, width), BF16),
            pltpu.VMEM((N_Y, ROWS, width), F32),
            pltpu.VMEM((2, hidden, width), BF16),
            pltpu.VMEM((2, 2, hidden, width), F32),
            pltpu.VMEM((2, hidden, width), BF16),
            pltpu.VMEM((2, hidden, width), BF16),
            pltpu.VMEM((2, N_Y // 2, hidden, 2 * ROWS), BF16),
            pltpu.VMEM((2, 7, HALF, width), BF16),
            pltpu.VMEM((2, 7, HALF, width), BF16),
            pltpu.VMEM((N_EXP, BLOCK, LANES), BF16),
            pltpu.VMEM((N_EXP, BLOCK, LANES), BF16),
            pltpu.VMEM((tokens, width), BF16),
            pltpu.VMEM((2, hidden, width), BF16),
            dma((5,)),
            dma((2, N_EXP)), dma((2, N_EXP)),
            dma((2, 8)), dma((2, 8)),
            dma((2, 2)), dma((2, 2)),
            dma((2, 2)), dma((2, 2)),
            dma((2, 7)), dma((2, 7)),
            dma((N_EXP,)), dma((N_EXP,)),
        ],
        compiler_params=pltpu.CompilerParams(
            collective_id=0, has_side_effects=True, vmem_limit_bytes=56 * 1024 * 1024
        ),
        name="moe_backward",
    )(
        x, g, gate.T, eid.T, slot.T, keep.T,
        jnp.swapaxes(weight_in[0], 0, 1), weight_out[0],
    )
    out, dwin, dwout = pl.pallas_call(
        hand_over, out_shape=shapes, in_specs=[vmem] * 3, out_specs=(vmem,) * 3, name="hand_over"
    )(*results)
    return out, jnp.swapaxes(dwin, 0, 1)[None], dwout[None]


def solution(mesh):
    split = P(("dp", "expert"), None)
    w_in, w_out = P("expert", None, "dp"), P("expert", "dp", None)
    return jax.shard_map(
        body, mesh=mesh, in_specs=(split,) * 6 + (w_in, w_out),
        out_specs=(split, w_in, w_out), check_vma=False,
    )
```
